256 devices in a mesh: group: 8 (over z_lo, y), dev: 32 (over x, z_hi, core).
Axes of the slice: x: 4, y: 4, z: 8 (z_hi: 4, z_lo: 2; z = z_hi * 2 + z_lo), core: 2. Of those that a mesh axis runs over, the one named last changes fastest.
Arguments:
- hidden_rows: bfloat16 [8192, 8192], P(('group', 'dev')), may hold values from -6 to 6
- norm_gain: float32 [8192], replicated, may hold values from 0.1 to 1.9
- query_weight: bfloat16 [8192, 8192], P('group', 'dev'), may hold values from -0.0625 to 0.0625
- key_weight: bfloat16 [8192, 1024], P('group'), may hold values from -0.0625 to 0.0625
- value_weight: bfloat16 [8192, 1024], P('group'), may hold values from -0.0625 to 0.0625
- packing: int32 [8, 1024], P('group'), may hold values from 0 to 1023, each once within a row
- segment_ids: int32 [8, 1024], P('group'), may hold values from 0 to 15, never falling along the last dimension, each value on 1 to 256 neighbouring positions
Outputs:
- context: bfloat16 [8192, 8192], P('group', 'dev')
The draws below stay inside these ranges and needn't reach their ends.
Inputs may be any that keep to these rules, and one draw needn't show every extreme that they name: Each row of packing holds every number below 1024 once. `segment_ids`: along each row segment numbers never fall; each response has 1 to 256 slots and one has exactly 256.
All inputs are finite; a program needn't handle non-finite values.
Results may differ from the reference program's by a relative error of at most 0.0076.
Values may be sent and summed in bfloat16 or wider, within the bound.
A program may use at most 128 MiB of HBM per device.

```python
import math
import jax
import jax.numpy as jnp
import numpy as np
from jax import lax

D = 8192
HEADS = 64
KV = 8
HDIM = 128
SEG_COUNT = 16
GROUP_TOK = 1024
ROWS = 8192
SEG_MOST = 256
N_GROUP = 8


def steps_of(stream_key, extent, shards, least, largest):
    level, own = 1.0, jax.random.fold_in(stream_key, 6)
    for dim, blocks in shards:
        heights = jnp.exp(jax.random.uniform(jax.random.fold_in(own, dim), (blocks,), jnp.float32, least / len(shards), largest / len(shards)))
        level = level * jnp.repeat(heights, extent[dim] // blocks).reshape([-1 if axis == dim else 1 for axis in range(len(extent))])
    return level


def length_profile(count, total, reach, skew):
    portions = [(1 << 20) // math.isqrt(rank ** skew) + 1 for rank in range(2, count + 1)]
    spare, counts = total - reach - (count - 1), [1] * (count - 1)
    while spare > 0:
        movable = [i for i in range(count - 1) if counts[i] < reach]
        pool, remaining = sum([portions[i] for i in movable]), spare
        for i in movable:
            more = min(reach - counts[i], max(1, remaining * portions[i] // pool), spare)
            counts[i] = counts[i] + more
            spare = spare - more
    return np.array([reach] + counts)


def uneven(key, number_of, total, most, lean):
    if number_of == 2:
        one = jax.random.randint(key, (), max(1, total - most), min(most, total - 1) + 1)
        return jnp.stack([one, total - one])
    lengths = jnp.asarray(length_profile(number_of, total, most, lean), jnp.int32)
    couples = (number_of - 1) // 2
    donor, receiver = lengths[1:1 + 2 * couples:2], lengths[2:2 + 2 * couples:2]
    margin = jnp.minimum(donor - 1, most - receiver)
    passed = jax.random.randint(jax.random.fold_in(key, 1), (couples,), 0, 1 << 20) % (margin + 1)
    lengths = lengths.at[1:1 + 2 * couples:2].set(donor - passed).at[2:2 + 2 * couples:2].set(receiver + passed)
    return lengths[jax.random.permutation(jax.random.fold_in(key, 2), number_of)]


def gaussian(rng, extent, scale, bound, pieces=(), kind=jnp.bfloat16):
    factor_of = steps_of(rng, extent, pieces, -0.22, 0.18) if pieces else 1.0
    entries = jax.random.normal(rng, extent, jnp.float32) * scale * factor_of
    return jnp.minimum(jnp.maximum(entries, -bound), bound).astype(kind)


def setup_inputs(seed: int = 0) -> dict:
    streams_of = jax.random.split(jax.random.key(seed), 8)
    return {
        "hidden_rows": gaussian(streams_of[0], (ROWS, D), 1.0, 6.0, ((0, 256),)),
        "norm_gain": jnp.clip(1.0 + 0.18 * jax.random.normal(streams_of[1], (D,), jnp.float32), 0.1, 1.9),
        "query_weight": gaussian(streams_of[2], (D, HEADS * HDIM), D ** -0.5, 0.0625, ((0, 8), (1, 32))),
        "key_weight": gaussian(streams_of[3], (D, KV * HDIM), D ** -0.5, 0.0625, ((0, 8),)),
        "value_weight": gaussian(streams_of[4], (D, KV * HDIM), D ** -0.5, 0.0625, ((0, 8),)),
        "packing": jax.vmap(lambda own: jax.random.permutation(own, GROUP_TOK))(jax.random.split(streams_of[5], N_GROUP)).reshape((N_GROUP, GROUP_TOK)).astype(jnp.int32),
        "segment_ids": jax.vmap(lambda own: jnp.searchsorted(jnp.cumsum(uneven(own, SEG_COUNT, GROUP_TOK, SEG_MOST, 2)), jnp.arange(GROUP_TOK), side="right"))(jax.random.split(streams_of[6], N_GROUP)).reshape((N_GROUP, GROUP_TOK)).astype(jnp.int32),
    }


def reference(hidden_rows, norm_gain, query_weight, key_weight, value_weight, packing, segment_ids):
    widened = hidden_rows.astype(jnp.float32)
    inverse = lax.rsqrt(lax.optimization_barrier(jnp.mean(widened * widened, axis=1, keepdims=True)) + 1e-06)
    normed = (widened * inverse * norm_gain).astype(jnp.bfloat16)
    groups = packing.shape[0]
    slots = packing.shape[1]
    offsets = (jnp.arange(groups, dtype=jnp.int32) * slots)[:, None]
    packed = normed[(packing + offsets).reshape(-1)]
    share = HEADS // KV
    query = jnp.dot(packed, query_weight, preferred_element_type=jnp.float32).astype(jnp.bfloat16)
    key_rows = jnp.dot(packed, key_weight, preferred_element_type=jnp.float32).astype(jnp.bfloat16)
    value_rows = jnp.dot(packed, value_weight, preferred_element_type=jnp.float32).astype(jnp.bfloat16)
    query = query.reshape(groups, slots, KV, share, HDIM)
    key_rows = key_rows.reshape(groups, slots, KV, HDIM)
    value_rows = value_rows.reshape(groups, slots, KV, HDIM)
    position = jnp.arange(slots, dtype=jnp.int32)

    def one_group(operand):
        group_query, group_keys, group_values, segment = operand
        allowed = (segment[:, None] == segment[None, :]) & (position[None, :] <= position[:, None])

        def one_head(inner):
            head_query, head_keys, head_values = inner
            scores = jnp.einsum('igd,jd->gij', head_query.astype(jnp.float32), head_keys.astype(jnp.float32)) / math.sqrt(HDIM)
            powers = jnp.where(allowed[None], jnp.exp(scores), 0.0)
            attend = (powers / lax.optimization_barrier(jnp.sum(powers, axis=2, keepdims=True))).astype(jnp.bfloat16)
            mixed = jnp.einsum('gij,jd->igd', attend.astype(jnp.float32), head_values.astype(jnp.float32))
            return mixed.astype(jnp.bfloat16)
        result = lax.map(one_head, (jnp.moveaxis(group_query, 1, 0), jnp.moveaxis(group_keys, 1, 0), jnp.moveaxis(group_values, 1, 0)))
        return jnp.moveaxis(result, 0, 1).reshape(slots, HEADS * HDIM)
    context = lax.map(one_group, (query, key_rows, value_rows, segment_ids))
    return context.reshape(groups * slots, HEADS * HDIM)
```

```python
import math

import jax
import jax.numpy as jnp
from jax import lax
from jax.experimental import pallas as pl
from jax.experimental.pallas import tpu as pltpu
from jax.sharding import PartitionSpec as P

HDIM = 128
MESH = pl.DeviceIdType.MESH
EPS = 1e-06
COPIES = 92
SHIFT = (0, 3, 1, 2)


def project_kernel(
    x_ref, gain_ref, wq_ref, wk_ref, wv_ref, out_ref, xbuf, wbuf, acc, send_sem, recv_sem, local_sem
):
    g = lax.axis_index("group")
    d = lax.axis_index("dev")
    zl, y = g // 4, g % 4
    x, zh, c = d // 8, (d // 2) % 4, d % 2
    rows = x_ref.shape[0]
    half = rows // 2
    slab = wq_ref.shape[0]
    wide = wq_ref.shape[1]

    def dev_at(dx, dz, core):
        return (((x + dx) % 4) * 4 + (zh + dz) % 4) * 2 + core

    right, left = (g, dev_at(1, 0, c)), (g, dev_at(3, 0, c))
    up, down = (g, dev_at(0, 1, c)), (g, dev_at(0, 3, c))
    sibling = (g, dev_at(0, 0, 1 - c))
    across = ((1 - zl) * 4 + y, d)
    north, south = (zl * 4 + (y + 1) % 4, d), (zl * 4 + (y + 3) % 4, d)

    barrier = pltpu.get_barrier_semaphore()
    partners = (right, left, up, down, sibling, across, north, south)
    for partner in partners:
        pl.semaphore_signal(barrier, inc=1, device_id=partner, device_id_type=MESH)

    def xslot(zr, xr, cr, h):
        return xbuf.at[pl.ds((((zr * 4 + xr) * 2 + cr) * 2 + h) * half, half), :]

    def slab_at(zlr, yr):
        zl_of = zl if zlr == 0 else 1 - zl
        return (zl_of * 4 + (y + SHIFT[yr]) % 4) * slab

    def wslot(zlr, yr, h):
        start = pl.multiple_of(slab_at(zlr, yr) + h * (slab // 2), slab // 2)
        return wbuf.at[pl.ds(start, slab // 2), pl.ds(0, wide + HDIM)]

    def kvslot(zlr, yr, h, which):
        start = pl.multiple_of(slab_at(zlr, yr) + h * (slab // 2), slab // 2)
        return wbuf.at[pl.ds(start, slab // 2), pl.ds(wide + which * HDIM, HDIM)]

    index = {}
    started = []

    def number(key):
        return index.setdefault(key, len(index))

    def describe(key, src, dst, device):
        i = number(key)
        return pltpu.make_async_remote_copy(
            src_ref=src,
            dst_ref=dst,
            send_sem=send_sem.at[i],
            recv_sem=recv_sem.at[i],
            device_id=device,
            device_id_type=MESH,
        )

    def send(key, src, dst, device):
        copy = describe(key, src, dst, device)
        copy.start()
        started.append(copy)

    def arrive(key, dst):
        describe(key, dst, dst, sibling).wait_recv()

    def share_x(zr, xr, h):
        send(("s", zr, xr, h), xslot(zr, xr, 0, h), xslot(zr, xr, 1, h), sibling)

    def share_kv(zlr, yr, h):
        send(("k", zlr, yr, h), kvslot(zlr, yr, h, 0), kvslot(zlr, yr, h, 1), sibling)

    def spread_x(zr, h):
        send(("r", zr, h), xslot(zr, 0, 0, h), xslot(zr, 1, 0, h), right)
        send(("l", zr, h), xslot(zr, 0, 0, h), xslot(zr, 2, 0, h), left)

    def from_left(zr, h):
        arrive(("r", zr, h), xslot(zr, 1, 0, h))
        if h == 0:
            send(("ro", zr), xslot(zr, 1, 0, 0), xslot(zr, 3, 0, 0), right)
        share_x(zr, 1, h)

    def from_right(zr, h):
        arrive(("l", zr, h), xslot(zr, 2, 0, h))
        if h == 1:
            send(("lo", zr), xslot(zr, 2, 0, 1), xslot(zr, 3, 0, 1), left)
        share_x(zr, 2, h)

    def from_opposite(zr):
        arrive(("ro", zr), xslot(zr, 3, 0, 0))
        share_x(zr, 3, 0)
        arrive(("lo", zr), xslot(zr, 3, 0, 1))
        share_x(zr, 3, 1)

    def spread_w(zlr, h):
        send(("n", zlr, h), wslot(zlr, 0, h), wslot(zlr, 0, h), north)
        send(("t", zlr, h), wslot(zlr, 0, h), wslot(zlr, 0, h), south)

    def from_south(zlr, h):
        arrive(("n", zlr, h), wslot(zlr, 1, h))
        if h == 0:
            send(("no", zlr), wslot(zlr, 1, 0), wslot(zlr, 1, 0), north)
        share_kv(zlr, 1, h)

    def from_north(zlr, h):
        arrive(("t", zlr, h), wslot(zlr, 2, h))
        if h == 1:
            send(("to", zlr), wslot(zlr, 2, 1), wslot(zlr, 2, 1), south)
        share_kv(zlr, 2, h)

    def from_far(zlr):
        arrive(("no", zlr), wslot(zlr, 3, 0))
        share_kv(zlr, 3, 0)
        arrive(("to", zlr), wslot(zlr, 3, 1))
        share_kv(zlr, 3, 1)

    def from_below(h):
        arrive(("u", h), xslot(1, 0, 0, h))
        if h == 0:
            send(("uo",), xslot(1, 0, 0, 0), xslot(3, 0, 0, 0), up)
        spread_x(1, h)
        share_x(1, 0, h)

    def from_above(h):
        arrive(("d", h), xslot(2, 0, 0, h))
        if h == 1:
            send(("do",), xslot(2, 0, 0, 1), xslot(3, 0, 0, 1), down)
        spread_x(2, h)
        share_x(2, 0, h)

    def from_across(h):
        arrive(("a", h), wslot(1, 0, h))
        spread_w(1, h)
        share_kv(1, 0, h)

    own = pl.multiple_of(slab_at(0, 0), slab)
    own_q = pltpu.make_async_copy(
        wq_ref, wbuf.at[pl.ds(own, slab), pl.ds(0, wide)], local_sem.at[0]
    )
    own_q.start()
    column = pl.multiple_of((d * (wide // HDIM) // 8) * HDIM, HDIM)

    def own_kv(source):
        return pltpu.make_async_copy(
            source.at[:, pl.ds(column, HDIM)],
            wbuf.at[pl.ds(own, slab), pl.ds(wide, HDIM)],
            local_sem.at[1],
        )

    @pl.when(c == 0)
    def _():
        own_kv(wk_ref).start()

    @pl.when(c == 1)
    def _():
        own_kv(wv_ref).start()

    widened = x_ref[...].astype(jnp.float32)
    inverse = lax.rsqrt(jnp.mean(widened * widened, axis=1, keepdims=True) + EPS)
    xbuf[pl.ds(0, half), :] = (widened[:half] * inverse[:half] * gain_ref[...]).astype(jnp.bfloat16)
    xbuf[pl.ds(half, half), :] = (widened[half:] * inverse[half:] * gain_ref[...]).astype(jnp.bfloat16)

    own_q.wait()
    own_kv(wk_ref).wait()
    pl.semaphore_wait(barrier, len(partners))

    send(("r", 0, 0), xslot(0, 0, 0, 0), xslot(0, 1, 0, 0), right)
    send(("l", 0, 1), xslot(0, 0, 0, 1), xslot(0, 2, 0, 1), left)
    send(("u", 0), xslot(0, 0, 0, 0), xslot(1, 0, 0, 0), up)
    send(("d", 1), xslot(0, 0, 0, 1), xslot(2, 0, 0, 1), down)
    send(("n", 0, 0), wslot(0, 0, 0), wslot(0, 0, 0), north)
    send(("t", 0, 1), wslot(0, 0, 1), wslot(0, 0, 1), south)
    send(("a", 0), wslot(0, 0, 0), wslot(0, 0, 0), across)
    send(("r", 0, 1), xslot(0, 0, 0, 1), xslot(0, 1, 0, 1), right)
    send(("l", 0, 0), xslot(0, 0, 0, 0), xslot(0, 2, 0, 0), left)
    send(("u", 1), xslot(0, 0, 0, 1), xslot(1, 0, 0, 1), up)
    send(("d", 0), xslot(0, 0, 0, 0), xslot(2, 0, 0, 0), down)
    send(("n", 0, 1), wslot(0, 0, 1), wslot(0, 0, 1), north)
    send(("t", 0, 0), wslot(0, 0, 0), wslot(0, 0, 0), south)
    send(("a", 1), wslot(0, 0, 1), wslot(0, 0, 1), across)
    for h in (0, 1):
        share_x(0, 0, h)
        share_kv(0, 0, h)

    from_left(0, 0)
    from_right(0, 1)
    from_south(0, 0)
    from_north(0, 1)
    from_left(0, 1)
    from_right(0, 0)
    from_below(0)
    from_above(1)
    from_south(0, 1)
    from_north(0, 0)
    from_opposite(0)
    from_across(0)
    from_below(1)
    from_above(0)
    from_left(1, 0)
    from_right(2, 1)
    from_across(1)
    from_far(0)
    from_right(1, 0)
    from_left(2, 1)
    arrive(("uo",), xslot(3, 0, 0, 0))
    spread_x(3, 0)
    share_x(3, 0, 0)
    arrive(("do",), xslot(3, 0, 0, 1))
    spread_x(3, 1)
    share_x(3, 0, 1)
    from_right(1, 1)
    from_left(2, 0)
    from_south(1, 0)
    from_north(1, 1)
    from_left(1, 1)
    from_right(2, 0)
    from_south(1, 1)
    from_north(1, 0)
    from_opposite(1)
    from_opposite(2)
    from_far(1)

    def shared_x(zr):
        for xr in range(4):
            for h in (0, 1):
                arrive(("s", zr, xr, h), xslot(zr, xr, 1, h))

    def project(zr):
        count = 8 * rows
        acc[...] = jnp.zeros_like(acc)

        def step(k, carry):
            at = pl.ds(pl.multiple_of(k * slab, slab), slab)
            acc[...] += jnp.dot(
                xbuf[pl.ds(zr * count, count), at], wbuf[at, :], preferred_element_type=jnp.float32
            )
            return carry

        lax.fori_loop(0, 8, step, 0)
        for xr in range(4):
            for cr in range(2):
                core = c if cr == 0 else 1 - c
                to = pl.multiple_of(dev_at(SHIFT[xr], SHIFT[zr], core) * rows, rows)
                out_ref[pl.ds(to, rows), :] = acc[pl.ds((xr * 2 + cr) * rows, rows), :].astype(
                    jnp.bfloat16
                )

    for zlr in range(2):
        for yr in range(4):
            for h in (0, 1):
                arrive(("k", zlr, yr, h), kvslot(zlr, yr, h, 1))
    shared_x(0)
    project(0)
    from_left(3, 0)
    from_right(3, 1)
    shared_x(1)
    project(1)
    from_left(3, 1)
    from_right(3, 0)
    shared_x(2)
    project(2)
    from_opposite(3)
    shared_x(3)
    project(3)
    for copy in started:
        copy.wait_send()


def project_rows(rows, gain, query_weight, key_weight, value_weight):
    tokens, width = rows.shape
    slab, wide = query_weight.shape
    packed = wide + 2 * HDIM
    return pl.pallas_call(
        project_kernel,
        out_shape=jax.ShapeDtypeStruct((32 * tokens, packed), jnp.bfloat16),
        in_specs=[
            pl.BlockSpec(memory_space=pltpu.VMEM),
            pl.BlockSpec(memory_space=pltpu.VMEM),
            pl.BlockSpec(memory_space=pl.ANY),
            pl.BlockSpec(memory_space=pl.ANY),
            pl.BlockSpec(memory_space=pl.ANY),
        ],
        out_specs=pl.BlockSpec(memory_space=pltpu.VMEM),
        scratch_shapes=[
            pltpu.VMEM((32 * tokens, width), jnp.bfloat16),
            pltpu.VMEM((width, packed), jnp.bfloat16),
            pltpu.VMEM((8 * tokens, packed), jnp.float32),
            pltpu.SemaphoreType.DMA((COPIES,)),
            pltpu.SemaphoreType.DMA((COPIES,)),
            pltpu.SemaphoreType.DMA((2,)),
        ],
        compiler_params=pltpu.CompilerParams(collective_id=0, has_side_effects=True),
        name="gather_project",
    )(rows, gain, query_weight, key_weight, value_weight)


def attend_kernel(packing_ref, segment_ref, qkv_ref, out_ref, packed):
    slots = qkv_ref.shape[0]
    heads = out_ref.shape[1] // HDIM
    core = lax.axis_index("dev") % 2
    block = 128
    chunk = 256
    order = jnp.transpose(jnp.broadcast_to(packing_ref[...], (block, slots)))
    segment = jnp.transpose(jnp.broadcast_to(segment_ref[...], (block, slots)))
    for start in range(0, slots, chunk):
        lane = lax.broadcasted_iota(jnp.int32, (chunk, block), 1)
        picked = order[start : start + chunk]
        onehot = jnp.concatenate(
            [
                jnp.where(picked == lane + at, 1.0, 0.0).astype(jnp.bfloat16)
                for at in range(0, slots, block)
            ],
            axis=1,
        )
        packed[pl.ds(start, chunk), :] = jnp.dot(
            onehot, qkv_ref[...], preferred_element_type=jnp.float32
        ).astype(jnp.bfloat16)
    first = packed[:, pl.ds(heads * HDIM, HDIM)]
    second = packed[:, pl.ds((heads + 1) * HDIM, HDIM)]
    keys = jnp.where(core == 0, first, second)
    values = jnp.where(core == 0, second, first)
    for start in range(0, slots, block):
        begin = max(0, start - 2 * block)
        span = start + block - begin
        query = jnp.concatenate(
            [packed[pl.ds(start, block), pl.ds(h * HDIM, HDIM)] for h in range(heads)], axis=0
        )
        scores = lax.dot_general(
            query,
            keys[begin : begin + span],
            (((1,), (1,)), ((), ())),
            preferred_element_type=jnp.float32,
        ) / math.sqrt(HDIM)
        own = jnp.concatenate([segment[start : start + block]] * (span // block), axis=1)
        other = segment_ref[:, pl.ds(begin, span)]
        slot = start + lax.broadcasted_iota(jnp.int32, (block, span), 0)
        key_slot = begin + lax.broadcasted_iota(jnp.int32, (block, span), 1)
        allowed = (own == other) & (key_slot <= slot)
        allowed = jnp.concatenate([allowed.astype(jnp.float32)] * heads, axis=0)
        powers = jnp.where(allowed > 0.5, jnp.exp(scores), 0.0)
        attend = (powers / jnp.sum(powers, axis=1, keepdims=True)).astype(jnp.bfloat16)
        mixed = jnp.dot(attend, values[begin : begin + span], preferred_element_type=jnp.float32)
        for h in range(heads):
            out_ref[pl.ds(start, block), pl.ds(h * HDIM, HDIM)] = mixed[
                h * block : (h + 1) * block
            ].astype(jnp.bfloat16)


def per_device(
    hidden_rows, norm_gain, query_weight, key_weight, value_weight, packing, segment_ids
):
    qkv = project_rows(hidden_rows, norm_gain[None, :], query_weight, key_weight, value_weight)
    slots, wide = qkv.shape[0], query_weight.shape[1]
    return pl.pallas_call(
        attend_kernel,
        out_shape=jax.ShapeDtypeStruct((slots, wide), jnp.bfloat16),
        in_specs=[pl.BlockSpec(memory_space=pltpu.VMEM)] * 3,
        out_specs=pl.BlockSpec(memory_space=pltpu.VMEM),
        scratch_shapes=[pltpu.VMEM(qkv.shape, jnp.bfloat16)],
        name="attend",
    )(packing, segment_ids, qkv)


def solution(mesh):
    in_specs = (
        P(("group", "dev"), None),
        P(),
        P("group", "dev"),
        P("group", None),
        P("group", None),
        P("group", None),
        P("group", None),
    )
    out_specs = P("group", "dev")
    return jax.shard_map(
        per_device, mesh=mesh, in_specs=in_specs, out_specs=out_specs, check_vma=False
    )
```

```python
import math

import jax
import jax.numpy as jnp
from jax import lax
from jax.experimental import pallas as pl
from jax.experimental.pallas import tpu as pltpu
from jax.sharding import PartitionSpec as P

HDIM = 128
MESH = pl.DeviceIdType.MESH
EPS = 1e-06
COPIES = 92
SHIFT = (0, 3, 1, 2)


def project_kernel(
    x_ref, gain_ref, wq_ref, wk_ref, wv_ref, out_ref, xbuf, wbuf, acc, send_sem, recv_sem, local_sem
):
    g = lax.axis_index("group")
    d = lax.axis_index("dev")
    zl, y = g // 4, g % 4
    x, zh, c = d // 8, (d // 2) % 4, d % 2
    rows = x_ref.shape[0]
    half = rows // 2
    slab = wq_ref.shape[0]
    wide = wq_ref.shape[1]

    def dev_at(dx, dz, core):
        return (((x + dx) % 4) * 4 + (zh + dz) % 4) * 2 + core

    right, left = (g, dev_at(1, 0, c)), (g, dev_at(3, 0, c))
    up, down = (g, dev_at(0, 1, c)), (g, dev_at(0, 3, c))
    sibling = (g, dev_at(0, 0, 1 - c))
    across = ((1 - zl) * 4 + y, d)
    north, south = (zl * 4 + (y + 1) % 4, d), (zl * 4 + (y + 3) % 4, d)

    barrier = pltpu.get_barrier_semaphore()
    partners = (right, left, up, down, sibling, across, north, south)
    for partner in partners:
        pl.semaphore_signal(barrier, inc=1, device_id=partner, device_id_type=MESH)

    def xslot(zr, xr, cr, h):
        return xbuf.at[pl.ds((((zr * 4 + xr) * 2 + cr) * 2 + h) * half, half), :]

    def slab_at(zlr, yr):
        zl_of = zl if zlr == 0 else 1 - zl
        return (zl_of * 4 + (y + SHIFT[yr]) % 4) * slab

    def wslot(zlr, yr, h):
        start = pl.multiple_of(slab_at(zlr, yr) + h * (slab // 2), slab // 2)
        return wbuf.at[pl.ds(start, slab // 2), pl.ds(0, wide + HDIM)]

    def kvslot(zlr, yr, h, which):
        start = pl.multiple_of(slab_at(zlr, yr) + h * (slab // 2), slab // 2)
        return wbuf.at[pl.ds(start, slab // 2), pl.ds(wide + which * HDIM, HDIM)]

    index = {}
    started = []

    def number(key):
        return index.setdefault(key, len(index))

    def describe(key, src, dst, device):
        i = number(key)
        return pltpu.make_async_remote_copy(
            src_ref=src,
            dst_ref=dst,
            send_sem=send_sem.at[i],
            recv_sem=recv_sem.at[i],
            device_id=device,
            device_id_type=MESH,
        )

    def send(key, src, dst, device):
        copy = describe(key, src, dst, device)
        copy.start()
        started.append(copy)

    def arrive(key, dst):
        describe(key, dst, dst, sibling).wait_recv()

    def share_x(zr, xr, h):
        send(("s", zr, xr, h), xslot(zr, xr, 0, h), xslot(zr, xr, 1, h), sibling)

    def share_kv(zlr, yr, h):
        send(("k", zlr, yr, h), kvslot(zlr, yr, h, 0), kvslot(zlr, yr, h, 1), sibling)

    def spread_x(zr, h):
        send(("r", zr, h), xslot(zr, 0, 0, h), xslot(zr, 1, 0, h), right)
        send(("l", zr, h), xslot(zr, 0, 0, h), xslot(zr, 2, 0, h), left)

    def from_left(zr, h):
        arrive(("r", zr, h), xslot(zr, 1, 0, h))
        if h == 0:
            send(("ro", zr), xslot(zr, 1, 0, 0), xslot(zr, 3, 0, 0), right)
        share_x(zr, 1, h)

    def from_right(zr, h):
        arrive(("l", zr, h), xslot(zr, 2, 0, h))
        if h == 1:
            send(("lo", zr), xslot(zr, 2, 0, 1), xslot(zr, 3, 0, 1), left)
        share_x(zr, 2, h)

    def from_opposite(zr):
        arrive(("ro", zr), xslot(zr, 3, 0, 0))
        share_x(zr, 3, 0)
        arrive(("lo", zr), xslot(zr, 3, 0, 1))
        share_x(zr, 3, 1)

    def spread_w(zlr, h):
        send(("n", zlr, h), wslot(zlr, 0, h), wslot(zlr, 0, h), north)
        send(("t", zlr, h), wslot(zlr, 0, h), wslot(zlr, 0, h), south)

    def from_south(zlr, h):
        arrive(("n", zlr, h), wslot(zlr, 1, h))
        if h == 0:
            send(("no", zlr), wslot(zlr, 1, 0), wslot(zlr, 1, 0), north)
        share_kv(zlr, 1, h)

    def from_north(zlr, h):
        arrive(("t", zlr, h), wslot(zlr, 2, h))
        if h == 1:
            send(("to", zlr), wslot(zlr, 2, 1), wslot(zlr, 2, 1), south)
        share_kv(zlr, 2, h)

    def from_far(zlr):
        arrive(("no", zlr), wslot(zlr, 3, 0))
        share_kv(zlr, 3, 0)
        arrive(("to", zlr), wslot(zlr, 3, 1))
        share_kv(zlr, 3, 1)

    def from_below(h):
        arrive(("u", h), xslot(1, 0, 0, h))
        if h == 0:
            send(("uo",), xslot(1, 0, 0, 0), xslot(3, 0, 0, 0), up)
        spread_x(1, h)
        share_x(1, 0, h)

    def from_above(h):
        arrive(("d", h), xslot(2, 0, 0, h))
        if h == 1:
            send(("do",), xslot(2, 0, 0, 1), xslot(3, 0, 0, 1), down)
        spread_x(2, h)
        share_x(2, 0, h)

    def from_across(h):
        arrive(("a", h), wslot(1, 0, h))
        spread_w(1, h)
        share_kv(1, 0, h)

    own = pl.multiple_of(slab_at(0, 0), slab)
    own_q = pltpu.make_async_copy(
        wq_ref, wbuf.at[pl.ds(own, slab), pl.ds(0, wide)], local_sem.at[0]
    )
    own_q.start()
    column = pl.multiple_of((d * (wide // HDIM) // 8) * HDIM, HDIM)

    def own_kv(source):
        return pltpu.make_async_copy(
            source.at[:, pl.ds(column, HDIM)],
            wbuf.at[pl.ds(own, slab), pl.ds(wide, HDIM)],
            local_sem.at[1],
        )

    @pl.when(c == 0)
    def _():
        own_kv(wk_ref).start()

    @pl.when(c == 1)
    def _():
        own_kv(wv_ref).start()

    widened = x_ref[...].astype(jnp.float32)
    inverse = lax.rsqrt(jnp.mean(widened * widened, axis=1, keepdims=True) + EPS)
    xbuf[pl.ds(0, half), :] = (widened[:half] * inverse[:half] * gain_ref[...]).astype(jnp.bfloat16)
    xbuf[pl.ds(half, half), :] = (widened[half:] * inverse[half:] * gain_ref[...]).astype(jnp.bfloat16)

    own_q.wait()
    own_kv(wk_ref).wait()
    pl.semaphore_wait(barrier, len(partners))

    send(("r", 0, 0), xslot(0, 0, 0, 0), xslot(0, 1, 0, 0), right)
    send(("l", 0, 1), xslot(0, 0, 0, 1), xslot(0, 2, 0, 1), left)
    send(("u", 0), xslot(0, 0, 0, 0), xslot(1, 0, 0, 0), up)
    send(("d", 1), xslot(0, 0, 0, 1), xslot(2, 0, 0, 1), down)
    send(("n", 0, 0), wslot(0, 0, 0), wslot(0, 0, 0), north)
    send(("t", 0, 1), wslot(0, 0, 1), wslot(0, 0, 1), south)
    send(("r", 0, 1), xslot(0, 0, 0, 1), xslot(0, 1, 0, 1), right)
    send(("l", 0, 0), xslot(0, 0, 0, 0), xslot(0, 2, 0, 0), left)
    send(("u", 1), xslot(0, 0, 0, 1), xslot(1, 0, 0, 1), up)
    send(("d", 0), xslot(0, 0, 0, 0), xslot(2, 0, 0, 0), down)
    send(("n", 0, 1), wslot(0, 0, 1), wslot(0, 0, 1), north)
    send(("t", 0, 0), wslot(0, 0, 0), wslot(0, 0, 0), south)
    for h in (0, 1):
        share_x(0, 0, h)
        share_kv(0, 0, h)

    send(("a", 0), wslot(0, 0, 0), wslot(0, 0, 0), across)
    send(("a", 1), wslot(0, 0, 1), wslot(0, 0, 1), across)
    from_left(0, 0)
    from_right(0, 1)
    from_south(0, 0)
    from_north(0, 1)
    from_below(0)
    from_above(1)
    from_left(0, 1)
    from_right(0, 0)
    from_south(0, 1)
    from_north(0, 0)
    from_opposite(0)
    from_left(1, 0)
    from_right(2, 1)
    from_below(1)
    from_above(0)
    from_right(1, 0)
    from_left(2, 1)
    from_far(0)
    from_across(0)
    from_across(1)
    from_left(1, 1)
    from_right(2, 0)
    from_right(1, 1)
    from_left(2, 0)
    arrive(("uo",), xslot(3, 0, 0, 0))
    spread_x(3, 0)
    share_x(3, 0, 0)
    arrive(("do",), xslot(3, 0, 0, 1))
    spread_x(3, 1)
    share_x(3, 0, 1)
    from_south(1, 0)
    from_north(1, 1)
    from_opposite(1)
    from_opposite(2)
    from_south(1, 1)
    from_north(1, 0)
    from_far(1)

    def shared_x(zr):
        for xr in range(4):
            for h in (0, 1):
                arrive(("s", zr, xr, h), xslot(zr, xr, 1, h))

    def project(zr):
        count = 8 * rows
        acc[...] = jnp.zeros_like(acc)

        def step(k, carry):
            at = pl.ds(pl.multiple_of(k * slab, slab), slab)
            acc[...] += jnp.dot(
                xbuf[pl.ds(zr * count, count), at], wbuf[at, :], preferred_element_type=jnp.float32
            )
            return carry

        lax.fori_loop(0, 8, step, 0)
        for xr in range(4):
            for cr in range(2):
                core = c if cr == 0 else 1 - c
                to = pl.multiple_of(dev_at(SHIFT[xr], SHIFT[zr], core) * rows, rows)
                out_ref[pl.ds(to, rows), :] = acc[pl.ds((xr * 2 + cr) * rows, rows), :].astype(
                    jnp.bfloat16
                )

    for zlr in range(2):
        for yr in range(4):
            for h in (0, 1):
                arrive(("k", zlr, yr, h), kvslot(zlr, yr, h, 1))
    shared_x(0)
    project(0)
    from_left(3, 0)
    from_right(3, 1)
    shared_x(1)
    project(1)
    from_left(3, 1)
    from_right(3, 0)
    shared_x(2)
    project(2)
    from_opposite(3)
    shared_x(3)
    project(3)
    for copy in started:
        copy.wait_send()


def project_rows(rows, gain, query_weight, key_weight, value_weight):
    tokens, width = rows.shape
    slab, wide = query_weight.shape
    packed = wide + 2 * HDIM
    return pl.pallas_call(
        project_kernel,
        out_shape=jax.ShapeDtypeStruct((32 * tokens, packed), jnp.bfloat16),
        in_specs=[
            pl.BlockSpec(memory_space=pltpu.VMEM),
            pl.BlockSpec(memory_space=pltpu.VMEM),
            pl.BlockSpec(memory_space=pl.ANY),
            pl.BlockSpec(memory_space=pl.ANY),
            pl.BlockSpec(memory_space=pl.ANY),
        ],
        out_specs=pl.BlockSpec(memory_space=pltpu.VMEM),
        scratch_shapes=[
            pltpu.VMEM((32 * tokens, width), jnp.bfloat16),
            pltpu.VMEM((width, packed), jnp.bfloat16),
            pltpu.VMEM((8 * tokens, packed), jnp.float32),
            pltpu.SemaphoreType.DMA((COPIES,)),
            pltpu.SemaphoreType.DMA((COPIES,)),
            pltpu.SemaphoreType.DMA((2,)),
        ],
        compiler_params=pltpu.CompilerParams(collective_id=0, has_side_effects=True),
        name="gather_project",
    )(rows, gain, query_weight, key_weight, value_weight)


def attend_kernel(packing_ref, segment_ref, qkv_ref, out_ref, packed):
    slots = qkv_ref.shape[0]
    heads = out_ref.shape[1] // HDIM
    core = lax.axis_index("dev") % 2
    block = 128
    chunk = 256
    order = jnp.transpose(jnp.broadcast_to(packing_ref[...], (block, slots)))
    segment = jnp.transpose(jnp.broadcast_to(segment_ref[...], (block, slots)))
    for start in range(0, slots, chunk):
        lane = lax.broadcasted_iota(jnp.int32, (chunk, block), 1)
        picked = order[start : start + chunk]
        onehot = jnp.concatenate(
            [
                jnp.where(picked == lane + at, 1.0, 0.0).astype(jnp.bfloat16)
                for at in range(0, slots, block)
            ],
            axis=1,
        )
        packed[pl.ds(start, chunk), :] = jnp.dot(
            onehot, qkv_ref[...], preferred_element_type=jnp.float32
        ).astype(jnp.bfloat16)
    first = packed[:, pl.ds(heads * HDIM, HDIM)]
    second = packed[:, pl.ds((heads + 1) * HDIM, HDIM)]
    keys = jnp.where(core == 0, first, second)
    values = jnp.where(core == 0, second, first)
    for start in range(0, slots, block):
        begin = max(0, start - 2 * block)
        span = start + block - begin
        query = jnp.concatenate(
            [packed[pl.ds(start, block), pl.ds(h * HDIM, HDIM)] for h in range(heads)], axis=0
        )
        scores = lax.dot_general(
            query,
            keys[begin : begin + span],
            (((1,), (1,)), ((), ())),
            preferred_element_type=jnp.float32,
        ) / math.sqrt(HDIM)
        own = jnp.concatenate([segment[start : start + block]] * (span // block), axis=1)
        other = segment_ref[:, pl.ds(begin, span)]
        slot = start + lax.broadcasted_iota(jnp.int32, (block, span), 0)
        key_slot = begin + lax.broadcasted_iota(jnp.int32, (block, span), 1)
        allowed = (own == other) & (key_slot <= slot)
        allowed = jnp.concatenate([allowed.astype(jnp.float32)] * heads, axis=0)
        powers = jnp.where(allowed > 0.5, jnp.exp(scores), 0.0)
        attend = (powers / jnp.sum(powers, axis=1, keepdims=True)).astype(jnp.bfloat16)
        mixed = jnp.dot(attend, values[begin : begin + span], preferred_element_type=jnp.float32)
        for h in range(heads):
            out_ref[pl.ds(start, block), pl.ds(h * HDIM, HDIM)] = mixed[
                h * block : (h + 1) * block
            ].astype(jnp.bfloat16)


def per_device(
    hidden_rows, norm_gain, query_weight, key_weight, value_weight, packing, segment_ids
):
    qkv = project_rows(hidden_rows, norm_gain[None, :], query_weight, key_weight, value_weight)
    slots, wide = qkv.shape[0], query_weight.shape[1]
    return pl.pallas_call(
        attend_kernel,
        out_shape=jax.ShapeDtypeStruct((slots, wide), jnp.bfloat16),
        in_specs=[pl.BlockSpec(memory_space=pltpu.VMEM)] * 3,
        out_specs=pl.BlockSpec(memory_space=pltpu.VMEM),
        scratch_shapes=[pltpu.VMEM(qkv.shape, jnp.bfloat16)],
        name="attend",
    )(packing, segment_ids, qkv)


def solution(mesh):
    in_specs = (
        P(("group", "dev"), None),
        P(),
        P("group", "dev"),
        P("group", None),
        P("group", None),
        P("group", None),
        P("group", None),
    )
    out_specs = P("group", "dev")
    return jax.shard_map(
        per_device, mesh=mesh, in_specs=in_specs, out_specs=out_specs, check_vma=False
    )
```

```python
import math

import jax
import jax.numpy as jnp
from jax import lax
from jax.experimental import pallas as pl
from jax.experimental.pallas import tpu as pltpu
from jax.sharding import PartitionSpec as P

HDIM = 128
MESH = pl.DeviceIdType.MESH
EPS = 1e-06
COPIES = 92
SHIFT = (0, 3, 1, 2)


def project_kernel(
    x_ref, gain_ref, wq_ref, wk_ref, wv_ref, out_ref, xbuf, wbuf, acc, send_sem, recv_sem, local_sem
):
    g = lax.axis_index("group")
    d = lax.axis_index("dev")
    zl, y = g // 4, g % 4
    x, zh, c = d // 8, (d // 2) % 4, d % 2
    rows = x_ref.shape[0]
    half = rows // 2
    slab = wq_ref.shape[0]
    wide = wq_ref.shape[1]

    def dev_at(dx, dz, core):
        return (((x + dx) % 4) * 4 + (zh + dz) % 4) * 2 + core

    right, left = (g, dev_at(1, 0, c)), (g, dev_at(3, 0, c))
    up, down = (g, dev_at(0, 1, c)), (g, dev_at(0, 3, c))
    sibling = (g, dev_at(0, 0, 1 - c))
    across = ((1 - zl) * 4 + y, d)
    north, south = (zl * 4 + (y + 1) % 4, d), (zl * 4 + (y + 3) % 4, d)

    barrier = pltpu.get_barrier_semaphore()
    partners = (right, left, up, down, sibling, across, north, south)
    for partner in partners:
        pl.semaphore_signal(barrier, inc=1, device_id=partner, device_id_type=MESH)

    def xslot(zr, xr, cr, h):
        return xbuf.at[pl.ds((((zr * 4 + xr) * 2 + cr) * 2 + h) * half, half), :]

    def slab_at(zlr, yr):
        zl_of = zl if zlr == 0 else 1 - zl
        return (zl_of * 4 + (y + SHIFT[yr]) % 4) * slab

    def wslot(zlr, yr, h):
        start = pl.multiple_of(slab_at(zlr, yr) + h * (slab // 2), slab // 2)
        return wbuf.at[pl.ds(start, slab // 2), pl.ds(0, wide + HDIM)]

    def kvslot(zlr, yr, h, which):
        start = pl.multiple_of(slab_at(zlr, yr) + h * (slab // 2), slab // 2)
        return wbuf.at[pl.ds(start, slab // 2), pl.ds(wide + which * HDIM, HDIM)]

    index = {}
    started = []

    def number(key):
        return index.setdefault(key, len(index))

    def describe(key, src, dst, device):
        i = number(key)
        return pltpu.make_async_remote_copy(
            src_ref=src,
            dst_ref=dst,
            send_sem=send_sem.at[i],
            recv_sem=recv_sem.at[i],
            device_id=device,
            device_id_type=MESH,
        )

    def send(key, src, dst, device):
        copy = describe(key, src, dst, device)
        copy.start()
        started.append(copy)

    def arrive(key, dst):
        describe(key, dst, dst, sibling).wait_recv()

    def share_x(zr, xr, h):
        send(("s", zr, xr, h), xslot(zr, xr, 0, h), xslot(zr, xr, 1, h), sibling)

    def share_kv(zlr, yr, h):
        send(("k", zlr, yr, h), kvslot(zlr, yr, h, 0), kvslot(zlr, yr, h, 1), sibling)

    def spread_x(zr, h):
        send(("r", zr, h), xslot(zr, 0, 0, h), xslot(zr, 1, 0, h), right)
        send(("l", zr, h), xslot(zr, 0, 0, h), xslot(zr, 2, 0, h), left)

    def from_left(zr, h):
        arrive(("r", zr, h), xslot(zr, 1, 0, h))
        if h == 0 and zr != 3:
            send(("ro", zr), xslot(zr, 1, 0, 0), xslot(zr, 3, 0, 0), right)
        share_x(zr, 1, h)

    def from_right(zr, h):
        arrive(("l", zr, h), xslot(zr, 2, 0, h))
        if h == 1 and zr != 3:
            send(("lo", zr), xslot(zr, 2, 0, 1), xslot(zr, 3, 0, 1), left)
        share_x(zr, 2, h)

    def from_opposite(zr, h):
        arrive((("ro", "lo")[h], zr), xslot(zr, 3, 0, h))
        if (zr, h) == (1, 0):
            send(("uc",), xslot(1, 3, 0, 0), xslot(3, 3, 0, 0), up)
        if (zr, h) == (2, 1):
            send(("dc",), xslot(2, 3, 0, 1), xslot(3, 3, 0, 1), down)
        share_x(zr, 3, h)

    def from_corner():
        arrive(("uc",), xslot(3, 3, 0, 0))
        share_x(3, 3, 0)
        arrive(("dc",), xslot(3, 3, 0, 1))
        share_x(3, 3, 1)

    def spread_w(zlr, h):
        send(("n", zlr, h), wslot(zlr, 0, h), wslot(zlr, 0, h), north)
        send(("t", zlr, h), wslot(zlr, 0, h), wslot(zlr, 0, h), south)

    def from_south(zlr, h):
        arrive(("n", zlr, h), wslot(zlr, 1, h))
        if h == 0:
            send(("no", zlr), wslot(zlr, 1, 0), wslot(zlr, 1, 0), north)
        share_kv(zlr, 1, h)

    def from_north(zlr, h):
        arrive(("t", zlr, h), wslot(zlr, 2, h))
        if h == 1:
            send(("to", zlr), wslot(zlr, 2, 1), wslot(zlr, 2, 1), south)
        share_kv(zlr, 2, h)

    def from_far(zlr):
        arrive(("no", zlr), wslot(zlr, 3, 0))
        share_kv(zlr, 3, 0)
        arrive(("to", zlr), wslot(zlr, 3, 1))
        share_kv(zlr, 3, 1)

    def from_below(h):
        arrive(("u", h), xslot(1, 0, 0, h))
        if h == 0:
            send(("uo",), xslot(1, 0, 0, 0), xslot(3, 0, 0, 0), up)
        spread_x(1, h)
        share_x(1, 0, h)

    def from_above(h):
        arrive(("d", h), xslot(2, 0, 0, h))
        if h == 1:
            send(("do",), xslot(2, 0, 0, 1), xslot(3, 0, 0, 1), down)
        spread_x(2, h)
        share_x(2, 0, h)

    def from_across(h):
        arrive(("a", h), wslot(1, 0, h))
        spread_w(1, h)
        share_kv(1, 0, h)

    def shared_x(zr):
        for xr in range(4):
            for h in (0, 1):
                arrive(("s", zr, xr, h), xslot(zr, xr, 1, h))

    def shared_kv(zlr):
        for yr in range(4):
            for h in (0, 1):
                arrive(("k", zlr, yr, h), kvslot(zlr, yr, h, 1))

    def project(zr, zlr):
        count = 8 * rows
        part = pl.ds(zr * count, count)
        first = (zl if zlr == 0 else 1 - zl) * 4
        if zlr == 0:
            acc[part, :] = jnp.zeros((count, acc.shape[1]), jnp.float32)

        def step(k, carry):
            at = pl.ds(pl.multiple_of((first + k) * slab, slab), slab)
            acc[part, :] += jnp.dot(
                xbuf[part, at], wbuf[at, :], preferred_element_type=jnp.float32
            )
            return carry

        lax.fori_loop(0, 4, step, 0)
        if zlr == 0:
            return
        for xr in range(4):
            for cr in range(2):
                core = c if cr == 0 else 1 - c
                to = pl.multiple_of(dev_at(SHIFT[xr], SHIFT[zr], core) * rows, rows)
                out_ref[pl.ds(to, rows), :] = acc[
                    pl.ds(zr * count + (xr * 2 + cr) * rows, rows), :
                ].astype(jnp.bfloat16)

    own = pl.multiple_of(slab_at(0, 0), slab)
    own_q = pltpu.make_async_copy(
        wq_ref, wbuf.at[pl.ds(own, slab), pl.ds(0, wide)], local_sem.at[0]
    )
    own_q.start()
    column = pl.multiple_of((d * (wide // HDIM) // 8) * HDIM, HDIM)

    def own_kv(source):
        return pltpu.make_async_copy(
            source.at[:, pl.ds(column, HDIM)],
            wbuf.at[pl.ds(own, slab), pl.ds(wide, HDIM)],
            local_sem.at[1],
        )

    @pl.when(c == 0)
    def _():
        own_kv(wk_ref).start()

    @pl.when(c == 1)
    def _():
        own_kv(wv_ref).start()

    widened = x_ref[...].astype(jnp.float32)
    inverse = lax.rsqrt(jnp.mean(widened * widened, axis=1, keepdims=True) + EPS)
    xbuf[pl.ds(0, half), :] = (widened[:half] * inverse[:half] * gain_ref[...]).astype(jnp.bfloat16)
    xbuf[pl.ds(half, half), :] = (widened[half:] * inverse[half:] * gain_ref[...]).astype(jnp.bfloat16)

    own_q.wait()
    own_kv(wk_ref).wait()
    pl.semaphore_wait(barrier, len(partners))

    send(("r", 0, 0), xslot(0, 0, 0, 0), xslot(0, 1, 0, 0), right)
    send(("l", 0, 1), xslot(0, 0, 0, 1), xslot(0, 2, 0, 1), left)
    send(("u", 0), xslot(0, 0, 0, 0), xslot(1, 0, 0, 0), up)
    send(("d", 1), xslot(0, 0, 0, 1), xslot(2, 0, 0, 1), down)
    send(("n", 0, 0), wslot(0, 0, 0), wslot(0, 0, 0), north)
    send(("t", 0, 1), wslot(0, 0, 1), wslot(0, 0, 1), south)
    send(("r", 0, 1), xslot(0, 0, 0, 1), xslot(0, 1, 0, 1), right)
    send(("l", 0, 0), xslot(0, 0, 0, 0), xslot(0, 2, 0, 0), left)
    send(("u", 1), xslot(0, 0, 0, 1), xslot(1, 0, 0, 1), up)
    send(("d", 0), xslot(0, 0, 0, 0), xslot(2, 0, 0, 0), down)
    send(("n", 0, 1), wslot(0, 0, 1), wslot(0, 0, 1), north)
    send(("t", 0, 0), wslot(0, 0, 0), wslot(0, 0, 0), south)
    for h in (0, 1):
        share_x(0, 0, h)
        share_kv(0, 0, h)

    send(("a", 0), wslot(0, 0, 0), wslot(0, 0, 0), across)
    send(("a", 1), wslot(0, 0, 1), wslot(0, 0, 1), across)
    from_left(0, 0)
    from_right(0, 1)
    from_south(0, 0)
    from_north(0, 1)
    from_below(0)
    from_above(1)
    from_left(0, 1)
    from_right(0, 0)
    from_south(0, 1)
    from_north(0, 0)
    from_opposite(0, 0)
    from_opposite(0, 1)
    from_left(1, 0)
    from_right(2, 1)
    from_below(1)
    from_above(0)
    from_right(1, 0)
    from_left(2, 1)
    from_far(0)
    from_across(0)
    from_across(1)
    from_left(1, 1)
    from_right(2, 0)
    from_right(1, 1)
    from_left(2, 0)
    arrive(("uo",), xslot(3, 0, 0, 0))
    spread_x(3, 0)
    share_x(3, 0, 0)
    arrive(("do",), xslot(3, 0, 0, 1))
    spread_x(3, 1)
    share_x(3, 0, 1)
    from_opposite(1, 0)
    from_opposite(2, 1)
    from_south(1, 0)
    from_north(1, 1)
    from_opposite(1, 1)
    from_opposite(2, 0)
    shared_kv(0)
    shared_x(0)
    project(0, 0)
    from_south(1, 1)
    from_north(1, 0)
    shared_x(1)
    project(1, 0)
    from_left(3, 0)
    from_right(3, 1)
    shared_x(2)
    project(2, 0)
    from_far(1)
    shared_kv(1)
    project(0, 1)
    from_left(3, 1)
    from_right(3, 0)
    project(1, 1)
    project(2, 1)
    from_corner()
    shared_x(3)
    project(3, 0)
    project(3, 1)
    for copy in started:
        copy.wait_send()


def project_rows(rows, gain, query_weight, key_weight, value_weight):
    tokens, width = rows.shape
    slab, wide = query_weight.shape
    packed = wide + 2 * HDIM
    return pl.pallas_call(
        project_kernel,
        out_shape=jax.ShapeDtypeStruct((32 * tokens, packed), jnp.bfloat16),
        in_specs=[
            pl.BlockSpec(memory_space=pltpu.VMEM),
            pl.BlockSpec(memory_space=pltpu.VMEM),
            pl.BlockSpec(memory_space=pl.ANY),
            pl.BlockSpec(memory_space=pl.ANY),
            pl.BlockSpec(memory_space=pl.ANY),
        ],
        out_specs=pl.BlockSpec(memory_space=pltpu.VMEM),
        scratch_shapes=[
            pltpu.VMEM((32 * tokens, width), jnp.bfloat16),
            pltpu.VMEM((width, packed), jnp.bfloat16),
            pltpu.VMEM((32 * tokens, packed), jnp.float32),
            pltpu.SemaphoreType.DMA((COPIES,)),
            pltpu.SemaphoreType.DMA((COPIES,)),
            pltpu.SemaphoreType.DMA((2,)),
        ],
        compiler_params=pltpu.CompilerParams(collective_id=0, has_side_effects=True),
        name="gather_project",
    )(rows, gain, query_weight, key_weight, value_weight)


def attend_kernel(packing_ref, segment_ref, qkv_ref, out_ref, packed):
    slots = qkv_ref.shape[0]
    heads = out_ref.shape[1] // HDIM
    core = lax.axis_index("dev") % 2
    block = 128
    chunk = 256
    order = jnp.transpose(jnp.broadcast_to(packing_ref[...], (block, slots)))
    segment = jnp.transpose(jnp.broadcast_to(segment_ref[...], (block, slots)))
    for start in range(0, slots, chunk):
        lane = lax.broadcasted_iota(jnp.int32, (chunk, block), 1)
        picked = order[start : start + chunk]
        onehot = jnp.concatenate(
            [
                jnp.where(picked == lane + at, 1.0, 0.0).astype(jnp.bfloat16)
                for at in range(0, slots, block)
            ],
            axis=1,
        )
        packed[pl.ds(start, chunk), :] = jnp.dot(
            onehot, qkv_ref[...], preferred_element_type=jnp.float32
        ).astype(jnp.bfloat16)
    first = packed[:, pl.ds(heads * HDIM, HDIM)]
    second = packed[:, pl.ds((heads + 1) * HDIM, HDIM)]
    keys = jnp.where(core == 0, first, second)
    values = jnp.where(core == 0, second, first)
    for start in range(0, slots, block):
        begin = max(0, start - 2 * block)
        span = start + block - begin
        query = jnp.concatenate(
            [packed[pl.ds(start, block), pl.ds(h * HDIM, HDIM)] for h in range(heads)], axis=0
        )
        scores = lax.dot_general(
            query,
            keys[begin : begin + span],
            (((1,), (1,)), ((), ())),
            preferred_element_type=jnp.float32,
        ) / math.sqrt(HDIM)
        own = jnp.concatenate([segment[start : start + block]] * (span // block), axis=1)
        other = segment_ref[:, pl.ds(begin, span)]
        slot = start + lax.broadcasted_iota(jnp.int32, (block, span), 0)
        key_slot = begin + lax.broadcasted_iota(jnp.int32, (block, span), 1)
        allowed = (own == other) & (key_slot <= slot)
        allowed = jnp.concatenate([allowed.astype(jnp.float32)] * heads, axis=0)
        powers = jnp.where(allowed > 0.5, jnp.exp(scores), 0.0)
        attend = (powers / jnp.sum(powers, axis=1, keepdims=True)).astype(jnp.bfloat16)
        mixed = jnp.dot(attend, values[begin : begin + span], preferred_element_type=jnp.float32)
        for h in range(heads):
            out_ref[pl.ds(start, block), pl.ds(h * HDIM, HDIM)] = mixed[
                h * block : (h + 1) * block
            ].astype(jnp.bfloat16)


def per_device(
    hidden_rows, norm_gain, query_weight, key_weight, value_weight, packing, segment_ids
):
    qkv = project_rows(hidden_rows, norm_gain[None, :], query_weight, key_weight, value_weight)
    slots, wide = qkv.shape[0], query_weight.shape[1]
    return pl.pallas_call(
        attend_kernel,
        out_shape=jax.ShapeDtypeStruct((slots, wide), jnp.bfloat16),
        in_specs=[pl.BlockSpec(memory_space=pltpu.VMEM)] * 3,
        out_specs=pl.BlockSpec(memory_space=pltpu.VMEM),
        scratch_shapes=[pltpu.VMEM(qkv.shape, jnp.bfloat16)],
        name="attend",
    )(packing, segment_ids, qkv)


def solution(mesh):
    in_specs = (
        P(("group", "dev"), None),
        P(),
        P("group", "dev"),
        P("group", None),
        P("group", None),
        P("group", None),
        P("group", None),
    )
    out_specs = P("group", "dev")
    return jax.shard_map(
        per_device, mesh=mesh, in_specs=in_specs, out_specs=out_specs, check_vma=False
    )
```

```python
import math

import jax
import jax.numpy as jnp
from jax import lax
from jax.experimental import pallas as pl
from jax.experimental.pallas import tpu as pltpu
from jax.sharding import PartitionSpec as P

HDIM = 128
MESH = pl.DeviceIdType.MESH
EPS = 1e-06
COPIES = 92
SHIFT = (0, 3, 1, 2)


def project_kernel(
    x_ref, gain_ref, wq_ref, wk_ref, wv_ref, out_ref, xbuf, wbuf, acc, send_sem, recv_sem, local_sem
):
    g = lax.axis_index("group")
    d = lax.axis_index("dev")
    zl, y = g // 4, g % 4
    x, zh, c = d // 8, (d // 2) % 4, d % 2
    rows = x_ref.shape[0]
    half = rows // 2
    slab = wq_ref.shape[0]
    wide = wq_ref.shape[1]

    def dev_at(dx, dz, core):
        return (((x + dx) % 4) * 4 + (zh + dz) % 4) * 2 + core

    right, left = (g, dev_at(1, 0, c)), (g, dev_at(3, 0, c))
    up, down = (g, dev_at(0, 1, c)), (g, dev_at(0, 3, c))
    sibling = (g, dev_at(0, 0, 1 - c))
    across = ((1 - zl) * 4 + y, d)
    north, south = (zl * 4 + (y + 1) % 4, d), (zl * 4 + (y + 3) % 4, d)

    barrier = pltpu.get_barrier_semaphore()
    partners = (right, left, up, down, sibling, across, north, south)
    for partner in partners:
        pl.semaphore_signal(barrier, inc=1, device_id=partner, device_id_type=MESH)

    def xslot(zr, xr, cr, h):
        return xbuf.at[pl.ds((((zr * 4 + xr) * 2 + cr) * 2 + h) * half, half), :]

    def slab_at(zlr, yr):
        zl_of = zl if zlr == 0 else 1 - zl
        return (zl_of * 4 + (y + SHIFT[yr]) % 4) * slab

    def wslot(zlr, yr, h):
        start = pl.multiple_of(slab_at(zlr, yr) + h * (slab // 2), slab // 2)
        return wbuf.at[pl.ds(start, slab // 2), pl.ds(0, wide + HDIM)]

    def kvslot(zlr, yr, h, which):
        start = pl.multiple_of(slab_at(zlr, yr) + h * (slab // 2), slab // 2)
        return wbuf.at[pl.ds(start, slab // 2), pl.ds(wide + which * HDIM, HDIM)]

    index = {}
    started = []

    def number(key):
        return index.setdefault(key, len(index))

    def describe(key, src, dst, device):
        i = number(key)
        return pltpu.make_async_remote_copy(
            src_ref=src,
            dst_ref=dst,
            send_sem=send_sem.at[i],
            recv_sem=recv_sem.at[i],
            device_id=device,
            device_id_type=MESH,
        )

    def send(key, src, dst, device):
        copy = describe(key, src, dst, device)
        copy.start()
        started.append(copy)

    def arrive(key, dst):
        describe(key, dst, dst, sibling).wait_recv()

    def share_x(zr, xr, h):
        send(("s", zr, xr, h), xslot(zr, xr, 0, h), xslot(zr, xr, 1, h), sibling)

    def share_kv(zlr, yr, h):
        send(("k", zlr, yr, h), kvslot(zlr, yr, h, 0), kvslot(zlr, yr, h, 1), sibling)

    def spread_x(zr, h):
        send(("r", zr, h), xslot(zr, 0, 0, h), xslot(zr, 1, 0, h), right)
        send(("l", zr, h), xslot(zr, 0, 0, h), xslot(zr, 2, 0, h), left)

    def from_left(zr, h):
        arrive(("r", zr, h), xslot(zr, 1, 0, h))
        if h == 0 and zr != 3:
            send(("ro", zr), xslot(zr, 1, 0, 0), xslot(zr, 3, 0, 0), right)
        share_x(zr, 1, h)

    def from_right(zr, h):
        arrive(("l", zr, h), xslot(zr, 2, 0, h))
        if h == 1 and zr != 3:
            send(("lo", zr), xslot(zr, 2, 0, 1), xslot(zr, 3, 0, 1), left)
        share_x(zr, 2, h)

    def from_opposite(zr, h):
        arrive((("ro", "lo")[h], zr), xslot(zr, 3, 0, h))
        if (zr, h) == (1, 0):
            send(("uc",), xslot(1, 3, 0, 0), xslot(3, 3, 0, 0), up)
        if (zr, h) == (2, 1):
            send(("dc",), xslot(2, 3, 0, 1), xslot(3, 3, 0, 1), down)
        share_x(zr, 3, h)

    def from_corner():
        arrive(("uc",), xslot(3, 3, 0, 0))
        share_x(3, 3, 0)
        arrive(("dc",), xslot(3, 3, 0, 1))
        share_x(3, 3, 1)

    def spread_w(zlr, h):
        send(("n", zlr, h), wslot(zlr, 0, h), wslot(zlr, 0, h), north)
        send(("t", zlr, h), wslot(zlr, 0, h), wslot(zlr, 0, h), south)

    def from_south(zlr, h):
        arrive(("n", zlr, h), wslot(zlr, 1, h))
        if h == 0:
            send(("no", zlr), wslot(zlr, 1, 0), wslot(zlr, 1, 0), north)
        share_kv(zlr, 1, h)

    def from_north(zlr, h):
        arrive(("t", zlr, h), wslot(zlr, 2, h))
        if h == 1:
            send(("to", zlr), wslot(zlr, 2, 1), wslot(zlr, 2, 1), south)
        share_kv(zlr, 2, h)

    def from_far(zlr):
        arrive(("no", zlr), wslot(zlr, 3, 0))
        share_kv(zlr, 3, 0)
        arrive(("to", zlr), wslot(zlr, 3, 1))
        share_kv(zlr, 3, 1)

    def from_below(h):
        arrive(("u", h), xslot(1, 0, 0, h))
        if h == 0:
            send(("uo",), xslot(1, 0, 0, 0), xslot(3, 0, 0, 0), up)
        spread_x(1, h)
        share_x(1, 0, h)

    def from_above(h):
        arrive(("d", h), xslot(2, 0, 0, h))
        if h == 1:
            send(("do",), xslot(2, 0, 0, 1), xslot(3, 0, 0, 1), down)
        spread_x(2, h)
        share_x(2, 0, h)

    def from_across(h):
        arrive(("a", h), wslot(1, 0, h))
        spread_w(1, h)
        share_kv(1, 0, h)

    def shared_x(zr):
        for xr in range(4):
            for h in (0, 1):
                arrive(("s", zr, xr, h), xslot(zr, xr, 1, h))

    def shared_kv(zlr):
        for yr in range(4):
            for h in (0, 1):
                arrive(("k", zlr, yr, h), kvslot(zlr, yr, h, 1))

    def project(zr, zlr):
        count = 8 * rows
        part = pl.ds(zr * count, count)
        first = (zl if zlr == 0 else 1 - zl) * 4
        if zlr == 0:
            acc[part, :] = jnp.zeros((count, acc.shape[1]), jnp.float32)

        def step(k, carry):
            at = pl.ds(pl.multiple_of((first + k) * slab, slab), slab)
            acc[part, :] += jnp.dot(
                xbuf[part, at], wbuf[at, :], preferred_element_type=jnp.float32
            )
            return carry

        lax.fori_loop(0, 4, step, 0)
        if zlr == 0:
            return
        for xr in range(4):
            for cr in range(2):
                core = c if cr == 0 else 1 - c
                to = pl.multiple_of(dev_at(SHIFT[xr], SHIFT[zr], core) * rows, rows)
                out_ref[pl.ds(to, rows), :] = acc[
                    pl.ds(zr * count + (xr * 2 + cr) * rows, rows), :
                ].astype(jnp.bfloat16)

    own = pl.multiple_of(slab_at(0, 0), slab)
    own_q = pltpu.make_async_copy(
        wq_ref, wbuf.at[pl.ds(own, slab), pl.ds(0, wide)], local_sem.at[0]
    )
    own_q.start()
    column = pl.multiple_of((d * (wide // HDIM) // 8) * HDIM, HDIM)

    def own_kv(source):
        return pltpu.make_async_copy(
            source.at[:, pl.ds(column, HDIM)],
            wbuf.at[pl.ds(own, slab), pl.ds(wide, HDIM)],
            local_sem.at[1],
        )

    @pl.when(c == 0)
    def _():
        own_kv(wk_ref).start()

    @pl.when(c == 1)
    def _():
        own_kv(wv_ref).start()

    widened = x_ref[...].astype(jnp.float32)
    inverse = lax.rsqrt(jnp.mean(widened * widened, axis=1, keepdims=True) + EPS)
    xbuf[pl.ds(0, half), :] = (widened[:half] * inverse[:half] * gain_ref[...]).astype(jnp.bfloat16)
    xbuf[pl.ds(half, half), :] = (widened[half:] * inverse[half:] * gain_ref[...]).astype(jnp.bfloat16)

    own_q.wait()
    own_kv(wk_ref).wait()
    pl.semaphore_wait(barrier, len(partners))

    send(("r", 0, 0), xslot(0, 0, 0, 0), xslot(0, 1, 0, 0), right)
    send(("l", 0, 1), xslot(0, 0, 0, 1), xslot(0, 2, 0, 1), left)
    send(("u", 0), xslot(0, 0, 0, 0), xslot(1, 0, 0, 0), up)
    send(("d", 1), xslot(0, 0, 0, 1), xslot(2, 0, 0, 1), down)
    send(("n", 0, 0), wslot(0, 0, 0), wslot(0, 0, 0), north)
    send(("t", 0, 1), wslot(0, 0, 1), wslot(0, 0, 1), south)
    send(("r", 0, 1), xslot(0, 0, 0, 1), xslot(0, 1, 0, 1), right)
    send(("l", 0, 0), xslot(0, 0, 0, 0), xslot(0, 2, 0, 0), left)
    send(("u", 1), xslot(0, 0, 0, 1), xslot(1, 0, 0, 1), up)
    send(("d", 0), xslot(0, 0, 0, 0), xslot(2, 0, 0, 0), down)
    send(("n", 0, 1), wslot(0, 0, 1), wslot(0, 0, 1), north)
    send(("t", 0, 0), wslot(0, 0, 0), wslot(0, 0, 0), south)
    for h in (0, 1):
        share_x(0, 0, h)
        share_kv(0, 0, h)

    send(("a", 0), wslot(0, 0, 0), wslot(0, 0, 0), across)
    send(("a", 1), wslot(0, 0, 1), wslot(0, 0, 1), across)
    from_left(0, 0)
    from_right(0, 1)
    from_south(0, 0)
    from_north(0, 1)
    from_below(0)
    from_above(1)
    from_left(0, 1)
    from_right(0, 0)
    from_south(0, 1)
    from_north(0, 0)
    from_opposite(0, 0)
    from_opposite(0, 1)
    from_left(1, 0)
    from_right(2, 1)
    from_below(1)
    from_above(0)
    from_right(1, 0)
    from_left(2, 1)
    from_far(0)
    from_across(0)
    from_across(1)
    from_left(1, 1)
    from_right(2, 0)
    from_right(1, 1)
    from_left(2, 0)
    arrive(("uo",), xslot(3, 0, 0, 0))
    spread_x(3, 0)
    share_x(3, 0, 0)
    arrive(("do",), xslot(3, 0, 0, 1))
    spread_x(3, 1)
    share_x(3, 0, 1)
    from_opposite(1, 0)
    from_opposite(2, 1)
    from_south(1, 0)
    from_north(1, 1)
    from_opposite(1, 1)
    from_opposite(2, 0)
    shared_kv(0)
    shared_x(0)
    project(0, 0)
    from_south(1, 1)
    from_north(1, 0)
    shared_x(1)
    project(1, 0)
    from_left(3, 0)
    from_right(3, 1)
    shared_x(2)
    project(2, 0)
    from_far(1)
    shared_kv(1)
    project(0, 1)
    from_left(3, 1)
    from_right(3, 0)
    project(1, 1)
    project(2, 1)
    from_corner()
    shared_x(3)
    project(3, 0)
    project(3, 1)
    for copy in started:
        copy.wait_send()


def project_rows(rows, gain, query_weight, key_weight, value_weight):
    tokens, width = rows.shape
    slab, wide = query_weight.shape
    packed = wide + 2 * HDIM
    return pl.pallas_call(
        project_kernel,
        out_shape=jax.ShapeDtypeStruct((32 * tokens, packed), jnp.bfloat16),
        in_specs=[
            pl.BlockSpec(memory_space=pltpu.VMEM),
            pl.BlockSpec(memory_space=pltpu.VMEM),
            pl.BlockSpec(memory_space=pl.ANY),
            pl.BlockSpec(memory_space=pl.ANY),
            pl.BlockSpec(memory_space=pl.ANY),
        ],
        out_specs=pl.BlockSpec(memory_space=pltpu.VMEM),
        scratch_shapes=[
            pltpu.VMEM((32 * tokens, width), jnp.bfloat16),
            pltpu.VMEM((width, packed), jnp.bfloat16),
            pltpu.VMEM((32 * tokens, packed), jnp.float32),
            pltpu.SemaphoreType.DMA((COPIES,)),
            pltpu.SemaphoreType.DMA((COPIES,)),
            pltpu.SemaphoreType.DMA((2,)),
        ],
        compiler_params=pltpu.CompilerParams(collective_id=0, has_side_effects=True),
        name="gather_project",
    )(rows, gain, query_weight, key_weight, value_weight)


def attend_kernel(packing_ref, segment_ref, qkv_ref, out_ref, packed):
    slots = qkv_ref.shape[0]
    heads = out_ref.shape[1] // HDIM
    core = lax.axis_index("dev") % 2
    block = 128
    chunk = 256
    order = jnp.transpose(jnp.broadcast_to(packing_ref[...], (block, slots)))
    segment = jnp.transpose(jnp.broadcast_to(segment_ref[...], (block, slots)))
    for start in range(0, slots, chunk):
        lane = lax.broadcasted_iota(jnp.int32, (chunk, block), 1)
        picked = order[start : start + chunk]
        onehot = jnp.concatenate(
            [
                jnp.where(picked == lane + at, 1.0, 0.0).astype(jnp.bfloat16)
                for at in range(0, slots, block)
            ],
            axis=1,
        )
        packed[pl.ds(start, chunk), :] = jnp.dot(
            onehot, qkv_ref[...], preferred_element_type=jnp.float32
        ).astype(jnp.bfloat16)
    first = packed[:, pl.ds(heads * HDIM, HDIM)]
    second = packed[:, pl.ds((heads + 1) * HDIM, HDIM)]
    keys = jnp.where(core == 0, first, second)
    values = jnp.where(core == 0, second, first)
    for start in range(0, slots, block):
        begin = max(0, start - 2 * block)
        span = start + block - begin
        query = jnp.concatenate(
            [packed[pl.ds(start, block), pl.ds(h * HDIM, HDIM)] for h in range(heads)], axis=0
        )
        scores = lax.dot_general(
            query,
            keys[begin : begin + span],
            (((1,), (1,)), ((), ())),
            preferred_element_type=jnp.float32,
        ) * (1.0 / math.sqrt(HDIM))
        own = jnp.concatenate([segment[start : start + block]] * (span // block), axis=1)
        other = segment_ref[:, pl.ds(begin, span)]
        slot = start + lax.broadcasted_iota(jnp.int32, (block, span), 0)
        key_slot = begin + lax.broadcasted_iota(jnp.int32, (block, span), 1)
        allowed = (own == other) & (key_slot <= slot)
        allowed = jnp.concatenate([allowed.astype(jnp.float32)] * heads, axis=0)
        powers = jnp.where(allowed > 0.5, jnp.exp(scores), 0.0)
        total = jnp.sum(powers, axis=1, keepdims=True)
        scale = jnp.where(total > 1e30, 0.0625, 1.0)
        inverse = 1.0 / (total * scale)
        attend = (powers * scale * inverse).astype(jnp.bfloat16)
        mixed = jnp.dot(attend, values[begin : begin + span], preferred_element_type=jnp.float32)
        for h in range(heads):
            out_ref[pl.ds(start, block), pl.ds(h * HDIM, HDIM)] = mixed[
                h * block : (h + 1) * block
            ].astype(jnp.bfloat16)


def per_device(
    hidden_rows, norm_gain, query_weight, key_weight, value_weight, packing, segment_ids
):
    qkv = project_rows(hidden_rows, norm_gain[None, :], query_weight, key_weight, value_weight)
    slots, wide = qkv.shape[0], query_weight.shape[1]
    return pl.pallas_call(
        attend_kernel,
        out_shape=jax.ShapeDtypeStruct((slots, wide), jnp.bfloat16),
        in_specs=[pl.BlockSpec(memory_space=pltpu.VMEM)] * 3,
        out_specs=pl.BlockSpec(memory_space=pltpu.VMEM),
        scratch_shapes=[pltpu.VMEM(qkv.shape, jnp.bfloat16)],
        name="attend",
    )(packing, segment_ids, qkv)


def solution(mesh):
    in_specs = (
        P(("group", "dev"), None),
        P(),
        P("group", "dev"),
        P("group", None),
        P("group", None),
        P("group", None),
        P("group", None),
    )
    out_specs = P("group", "dev")
    return jax.shard_map(
        per_device, mesh=mesh, in_specs=in_specs, out_specs=out_specs, check_vma=False
    )
```
